32 devices in a mesh: gene: 4 (over x, core), site: 8 (over z, y).
Axes of the slice: x: 2, y: 2, z: 4, core: 2. Of those that a mesh axis runs over, the one named last changes fastest.
Arguments:
- tips: bfloat16 [4, 32, 20, 16384], P('gene', None, None, 'site'), may hold values from 0.0009994507 to 1
- exchange: float32 [20, 20], replicated, may hold values from 0.05 to 5
- freqs: float32 [20], replicated, may hold values from 0.02 to 0.12
- rates: float32 [4], replicated, may hold values from 0.1 to 3
- branch: float32 [62], replicated, may hold values from 0.02 to 0.6
- children: int32 [31, 2], replicated, may hold values from 0 to 61, as said below
- slot_gene: int32 [4, 128], P('gene', 'site'), may hold values from 0 to 63, as said below
- site_count: int32 [4, 128], P('gene', 'site'), may hold values from 0 to 128, as said below
Outputs:
- site_loglik: float32 [4, 16384], P('gene', 'site')
- gene_loglik: float32 [4, 64], P('gene')
- total: float32 [], replicated
The draws below stay inside these ranges and needn't reach their ends.
Inputs may be any that keep to these rules, and one draw needn't show every extreme that they name: `children`: internal nodes come in 5 levels: the first 16 pair up all leaves, each next level pairs up all nodes of the level before, in node order; each node is a child once. On each device along site the slots with site_count > 0 come first; each device holds at least (64 + 8 - 1) // 8 of them and in each group one device has all 16 live; a live slot's live sites are its first ones. `slot_gene`: every gene of a group owns at least one live slot; on slots that are not live the value is 0.
All inputs are finite; a program needn't handle non-finite values.
Results may differ from the reference program's by a relative error of at most 0.0003.
Values may be sent and summed in bfloat16 or wider, within the bound.
No kernel may reach another device: no remote copies, remote signals or barrier semaphores. Data moves between devices by JAX's collectives and lax.ppermute only.
A program may use at most 128 MiB of HBM per device.

```python
import math
import jax
import jax.numpy as jnp
from jax import lax

STATES = 20
RATES = 4
LEVELS = 5
TILE = 128
SLOTS_DEV = 16
GROUP_GENES = 64
TAXA = 32
NODES = 62
SLOTS = 128
SITES = 16384
N_GENE = 4
N_SITE = 8


def slot_layout(key):
    keys = jax.random.split(jax.random.fold_in(key, 7), 6)
    draws = jax.random.randint(keys[0], (N_GENE, N_SITE), 0, SLOTS_DEV + 1)
    lowest = (GROUP_GENES + N_SITE - 1) // N_SITE
    live = jnp.maximum(lowest, draws * draws // SLOTS_DEV)
    fullest = jax.random.randint(keys[1], (N_GENE,), 0, N_SITE)
    live = jnp.where(jnp.arange(N_SITE)[None, :] == fullest[:, None], SLOTS_DEV, live)
    alive = (jnp.arange(SLOTS_DEV)[None, None, :] < live[:, :, None]).reshape(N_GENE, SLOTS)
    index = jnp.arange(SLOTS, dtype=jnp.int32)[None, :]
    score = jax.random.randint(keys[2], (N_GENE, SLOTS), 0, 2 ** 19) * SLOTS + index
    score = jnp.where(alive, score, 2 ** 19 * SLOTS + index)
    order = jnp.argsort(score, axis=1)
    ranked = jnp.argsort(order, axis=1).astype(jnp.int32)
    others = jax.random.randint(keys[3], (N_GENE, SLOTS), 0, GROUP_GENES)
    owner = jnp.where(alive, jnp.where(ranked < GROUP_GENES, ranked, others), 0)
    partial_value = jax.random.randint(keys[4], (N_GENE, SLOTS), 1, TILE + 1)
    pick = jax.random.randint(keys[5], (N_GENE, SLOTS), 0, 4) == 0
    sizes = jnp.where(alive, jnp.where(pick, partial_value, TILE), 0)
    return (owner.astype(jnp.int32), sizes.astype(jnp.int32))


def draw_slot_gene(key, part):
    return slot_layout(key)[0]


def draw_site_count(key, part):
    return slot_layout(key)[1]


def draw_children(key, part):
    rows = []
    prev_start = 0
    next_id = TAXA
    count = TAXA
    for level in range(LEVELS):
        order = jax.random.permutation(jax.random.fold_in(key, 100 + level), count) + prev_start
        rows.append(order.reshape(count // 2, 2))
        prev_start = next_id
        next_id = next_id + count // 2
        count = count // 2
    return jnp.concatenate(rows, axis=0).astype(jnp.int32)


def level_of(rng, shape, shards, least, top_value):
    def one(axis_at, blocks):
        heights = jax.random.uniform(jax.random.fold_in(jax.random.fold_in(rng, 6), axis_at), (blocks,), jnp.float32, least / len(shards), top_value / len(shards))
        return jnp.repeat(jnp.exp(heights), shape[axis_at] // blocks).reshape((-1,) + (1,) * (len(shape) - axis_at - 1))

    factor_of = one(*shards[0])
    for cut in shards[1:]:
        factor_of = factor_of * one(*cut)
    return factor_of


def setup_inputs(seed: int = 0) -> dict:
    key_of = jax.random.split(jax.random.key(seed), 9)
    return {
        "tips": jnp.clip(jnp.exp(math.log(1.0) - 6.9083047 * jax.random.uniform(key_of[0], (N_GENE, TAXA, STATES, SITES), jnp.float32) ** level_of(key_of[0], (N_GENE, TAXA, STATES, SITES), ((0, 4), (3, 8)), -0.2, 0.2)), 0.0009994507, 1.0).astype(jnp.bfloat16),
        "exchange": jnp.clip(jnp.exp(jax.random.uniform(key_of[1], (STATES, STATES), jnp.float32, math.log(0.05), math.log(5.0))), 0.05, 5.0),
        "freqs": jnp.clip(jnp.exp(jax.random.uniform(key_of[2], (STATES,), jnp.float32, math.log(0.02), math.log(0.12))), 0.02, 0.12),
        "rates": jnp.clip(jnp.exp(jax.random.uniform(key_of[3], (RATES,), jnp.float32, math.log(0.1), math.log(3.0))), 0.1, 3.0),
        "branch": jnp.clip(jnp.exp(jax.random.uniform(key_of[4], (NODES,), jnp.float32, math.log(0.02), math.log(0.6))), 0.02, 0.6),
        "children": draw_children(jax.random.fold_in(key_of[8], 71), 0),
        "slot_gene": draw_slot_gene(jax.random.fold_in(key_of[8], 71), 0),
        "site_count": draw_site_count(jax.random.fold_in(key_of[8], 71), 0),
    }


def transitions(exchange, freqs, rates, branch):
    eye = jnp.eye(STATES, dtype=jnp.float32)
    sym = (exchange + exchange.T) * 0.5 * (1.0 - eye)
    pi = freqs / jnp.sum(freqs)
    qmat = sym * pi[None, :]
    qmat = qmat - eye * jnp.sum(qmat, axis=1)[:, None]
    qmat = qmat / (-jnp.sum(pi * jnp.diagonal(qmat)))
    scaled = rates / jnp.mean(rates)
    times = (branch[:, None] * scaled[None, :]).reshape(-1) / 256.0
    amat = qmat[:, :, None] * times[None, None, :]
    term = amat
    power = eye[:, :, None] + amat
    for order in range(2, 9):
        term = jnp.einsum("ijb,jkb->ikb", term, amat, precision=lax.Precision.HIGHEST) / order
        power = power + term
    for step in range(8):
        power = jnp.einsum("ijb,jkb->ikb", power, power, precision=lax.Precision.HIGHEST)
    return power.transpose(2, 0, 1).reshape(NODES, RATES, STATES, STATES), pi


def prune(leaves, children, pmat, pi):
    width = leaves.shape[-1]
    level_x = leaves
    level_scale = jnp.zeros((TAXA, width), jnp.float32)
    prev_start = 0
    row_start = 0
    count = TAXA
    for level in range(LEVELS):
        half = count // 2
        pairs = children[row_start:row_start + half]
        left_id = pairs[:, 0]
        right_id = pairs[:, 1]
        left_x = jnp.take(level_x, left_id - prev_start, axis=0)
        right_x = jnp.take(level_x, right_id - prev_start, axis=0)
        left_p = jnp.take(pmat, left_id, axis=0)
        right_p = jnp.take(pmat, right_id, axis=0)
        if level == 0:
            left_y = jnp.einsum("nkij,njs->nkis", left_p, left_x, precision=lax.Precision.HIGHEST)
            right_y = jnp.einsum("nkij,njs->nkis", right_p, right_x, precision=lax.Precision.HIGHEST)
        else:
            left_y = jnp.einsum("nkij,nkjs->nkis", left_p, left_x, precision=lax.Precision.HIGHEST)
            right_y = jnp.einsum("nkij,nkjs->nkis", right_p, right_x, precision=lax.Precision.HIGHEST)
        product = left_y * right_y
        top = jnp.max(product, axis=(1, 2))
        level_x = product / top[:, None, None]
        level_scale = jnp.log(top) + jnp.take(level_scale, left_id - prev_start, axis=0) + jnp.take(level_scale, right_id - prev_start, axis=0)
        prev_start = TAXA + row_start
        row_start = row_start + half
        count = half
    lik = jnp.sum(level_x[0] * pi[None, :, None], axis=(0, 1)) / RATES
    return jnp.log(lik) + level_scale[0]


def reference(tips, exchange, freqs, rates, branch, children, slot_gene, site_count):
    pmat, pi = transitions(exchange, freqs, rates, branch)
    block = 4 * TILE
    per_group = SITES // block
    zero = jnp.zeros((), jnp.int32)

    def one_block(index):
        group = (index // per_group).astype(jnp.int32)
        start = ((index % per_group) * block).astype(jnp.int32)
        piece = lax.dynamic_slice(tips, (group, zero, zero, start), (1, TAXA, STATES, block))[0]
        return prune(piece.astype(jnp.float32), children, pmat, pi)

    values = lax.map(one_block, jnp.arange(N_GENE * per_group, dtype=jnp.int32))
    values = values.reshape(N_GENE, SLOTS, TILE)
    inside = jnp.arange(TILE, dtype=jnp.int32)[None, None, :] < site_count[:, :, None]
    values = jnp.where(inside, values, 0.0)
    site_loglik = values.reshape(N_GENE, SITES)
    per_slot = jnp.sum(values, axis=2)
    genes = jnp.arange(GROUP_GENES, dtype=jnp.int32)
    hit = ((slot_gene[:, None, :] == genes[None, :, None]) & (site_count[:, None, :] > 0)).astype(jnp.float32)
    sums = jnp.sum(hit * per_slot[:, None, :], axis=2)
    counts = jnp.sum(hit * site_count.astype(jnp.float32)[:, None, :], axis=2)
    gene_loglik = sums / counts
    total = jnp.sum(per_slot) / (TILE * SLOTS)
    return site_loglik, gene_loglik, total
```

```python
import functools

import jax
import jax.numpy as jnp
from jax import lax
from jax.experimental import pallas as pl
from jax.experimental.pallas import tpu as pltpu
from jax.sharding import PartitionSpec as P

GROUP_GENES = 64
TAYLOR = 8
SQUARINGS = 8
LANES = 128
F32 = jnp.float32
BF16 = jnp.bfloat16


def up(value, to):
    return (value + to - 1) // to * to


def kernel(
    dims,
    children,
    counts,
    genes,
    exchange,
    freqs,
    rates,
    branch,
    tips,
    site_out,
    part_out,
    leaves,
    mat_a,
    mat_b,
    leaf_f,
    inner_f,
    leaf_p,
    inner_p,
    partial,
    scale,
    sems,
):
    taxa, states, cats, width, slots = dims
    pad = up(states, 8)
    half = leaf_p.shape[2] // 4
    rows = states * cats
    slot_n = 64
    batch = cats * slot_n
    copy = pltpu.make_async_copy(tips.at[0], leaves, sems.at[0])
    copy.start()

    row = lax.broadcasted_iota(jnp.int32, (states, states), 0)
    col = lax.broadcasted_iota(jnp.int32, (states, states), 1)
    eye = (row == col).astype(F32)
    sym = (exchange[...] + exchange[...].T) * 0.5 * (1.0 - eye)
    pi = freqs[...] / jnp.sum(freqs[...], axis=1, keepdims=True)
    qmat = sym * pi
    qmat = qmat - eye * jnp.sum(qmat, axis=1, keepdims=True)
    rate = -jnp.sum(jnp.sum(qmat * eye * pi, axis=1, keepdims=True), axis=0, keepdims=True)
    qmat = qmat / rate
    scaled = rates[...] / jnp.mean(rates[...], axis=1, keepdims=True)
    lengths = jnp.concatenate(
        [branch[...], jnp.zeros((1, slot_n - branch.shape[1]), F32)], axis=1
    )
    times = jnp.concatenate([lengths * scaled[:, k : k + 1] for k in range(cats)], axis=1)
    times = times / 256.0

    base = qmat.T
    powers = [base]
    dot = functools.partial(jnp.dot, precision=lax.Precision.HIGHEST, preferred_element_type=F32)
    for order in range(2, TAYLOR + 1):
        lo = order // 2
        powers.append(dot(powers[lo - 1], powers[order - lo - 1]))
    fill = jnp.zeros((pad - states, states), F32)
    powers = [jnp.concatenate([p, fill], axis=0) for p in powers]
    times_b = jnp.broadcast_to(times, (pad, batch))
    for i in range(states):
        acc = jnp.zeros((pad, batch), F32)
        for order in range(TAYLOR, 0, -1):
            column = jnp.broadcast_to(powers[order - 1][:, i : i + 1], (pad, batch))
            acc = (column + acc) * (times_b * (1.0 / order))
        mat_a[i] = acc

    block = 4

    def square(src, dst):
        def rows_of(ib, carry):
            first = ib * block
            acc = []
            for q in range(block):
                acc.append(src[first + q] * 2.0)
            for j in range(states):
                right = src[j]
                for q in range(block):
                    acc[q] = acc[q] + src[first + q, pl.ds(j, 1), :] * right
            for q in range(block):
                dst[first + q] = acc[q]
            return carry

        lax.fori_loop(0, states // block, rows_of, 0)

    def twice(step, carry):
        square(mat_a, mat_b)
        square(mat_b, mat_a)
        return carry

    lax.fori_loop(0, SQUARINGS // 2, twice, 0)

    sub = lax.broadcasted_iota(jnp.int32, (pad, LANES), 0)
    quarter = slot_n // 2

    def spread(i, carry):
        one = (sub == i).astype(F32)
        for h in range(batch // LANES):
            x = mat_a[i, :, pl.ds(h * LANES, LANES)] + one
            z = jnp.concatenate([x, jnp.zeros((LANES - pad, LANES), F32)], axis=0).T
            for g in range(LANES // slot_n):
                k = h * (LANES // slot_n) + g
                to = pl.ds(k * states + i, quarter, stride=rows)
                leaf_f[to, :] = z[g * slot_n : g * slot_n + quarter]
                inner = z[g * slot_n + quarter : (g + 1) * slot_n]
                inner_f[to, :] = pltpu.roll(inner, k * states, 1) if k else inner
        return carry

    lax.fori_loop(0, states, spread, 0)

    lane = lax.broadcasted_iota(jnp.int32, (rows, LANES), 1)

    def split(n, carry):
        at = pl.ds(pl.multiple_of(n * rows, 8), rows)
        x = leaf_f[at, :]
        hi = x.astype(BF16).astype(F32)
        leaf_p[n] = (hi + pltpu.roll(x - hi, half, 1)).astype(BF16)
        x = inner_f[at, :]
        hi = x.astype(BF16).astype(F32)
        turned = pltpu.roll(hi, rows, 1)
        first = jnp.where(lane < rows, hi, turned)
        second = jnp.where(lane < 2 * rows - LANES, turned, pltpu.roll(x - hi, 2 * rows - LANES, 1))
        inner_p[n] = jnp.concatenate([first, second], axis=1).astype(BF16)
        return carry

    lax.fori_loop(0, taxa, split, 0)

    copy.wait()
    scale[...] = jnp.zeros_like(scale)
    chunk = 256

    def store(node, cols, p):
        hi = p.astype(BF16)
        lo = (p - hi.astype(F32)).astype(BF16)
        partial[node, pl.ds(0, rows), cols] = hi
        partial[node, pl.ds(rows, rows), cols] = lo
        partial[node, pl.ds(2 * rows, rows), cols] = hi

    def message(child, cols, leaf):
        if leaf:
            x = leaves[child, :, cols]
            gap = jnp.zeros((half - states, chunk), BF16)
            x = jnp.concatenate([x, gap, x, gap], axis=0)
            return jnp.dot(leaf_p[child, :, : 2 * half], x, preferred_element_type=F32)
        inner = child - taxa
        return jnp.dot(
            inner_p[inner, :, : 3 * rows], partial[inner, :, cols], preferred_element_type=F32
        )

    def node_at(node, leaf, rescale):
        left, right = children[node, 0], children[node, 1]
        for c in range(width // chunk):
            cols = pl.ds(c * chunk, chunk)
            p = message(left, cols, leaf) * message(right, cols, leaf)
            if rescale:
                top = jnp.max(p, axis=0, keepdims=True)
                p = p * (1.0 / top)
                scale[:, cols] = scale[:, cols] + jnp.log(top)
            store(node, cols, p)

    first, count, level = 0, taxa // 2, 0
    while count > 1:

        def at_node(node, carry, level=level):
            node_at(node, level == 0, level % 3 == 2)
            return carry

        lax.fori_loop(first, first + count, at_node, 0)
        first, count, level = first + count, count // 2, level + 1

    wide = lax.broadcasted_iota(jnp.int32, (rows, states), 0)
    tall = lax.broadcasted_iota(jnp.int32, (rows, states), 1)
    weight = jnp.where(wide % states == tall, pi, 0.0)
    weight = jnp.sum(weight, axis=1, keepdims=True) / cats
    left, right = children[first, 0], children[first, 1]
    line = lax.broadcasted_iota(jnp.int32, (1, LANES), 1)
    tile = width // slots
    sums = jnp.zeros((1, LANES), F32)
    sizes = jnp.zeros((1, LANES), F32)
    whole = jnp.zeros((1, 1), F32)
    for c in range(width // chunk):
        cols = pl.ds(c * chunk, chunk)
        p = message(left, cols, False) * message(right, cols, False)
        lik = jnp.sum(p * weight, axis=0, keepdims=True)
        value = jnp.log(lik) + scale[:, cols]
        for t in range(chunk // tile):
            slot = c * (chunk // tile) + t
            size = counts[0, slot]
            part = jnp.where(line < size, value[:, t * tile : (t + 1) * tile], 0.0)
            site_out[:, pl.ds(slot * tile, tile)] = part
            sum_of = jnp.sum(part, axis=1, keepdims=True)
            hit = (line == genes[0, slot]) & (size > 0)
            sums = sums + jnp.where(hit, sum_of, 0.0)
            sizes = sizes + jnp.where(hit, size.astype(F32), 0.0)
            whole = whole + sum_of
    tail = jnp.where(line == 0, whole, 0.0)
    message_row = jnp.concatenate([sums, sizes, tail], axis=1)
    part_out[...] = jnp.broadcast_to(message_row, part_out.shape)


def on_device(tips, exchange, freqs, rates, branch, children, slot_gene, site_count):
    taxa, states, width = tips.shape[1:]
    slots = site_count.shape[1]
    cats = rates.shape[0]
    rows = states * cats
    half = 32
    members = lax.axis_size("site")
    groups = lax.axis_size("gene")
    devices = members * groups
    pad = up(states, 8)
    smem = pl.BlockSpec(memory_space=pltpu.SMEM)
    vmem = pl.BlockSpec(memory_space=pltpu.VMEM)
    site, part = pl.pallas_call(
        functools.partial(kernel, (taxa, states, cats, width, slots)),
        out_shape=(
            jax.ShapeDtypeStruct((1, width), F32),
            jax.ShapeDtypeStruct((devices, 3 * LANES), F32),
        ),
        in_specs=[smem] * 3 + [vmem] * 4 + [pl.BlockSpec(memory_space=pl.ANY)],
        out_specs=(vmem, vmem),
        scratch_shapes=[
            pltpu.VMEM((taxa, states, width), BF16),
            pltpu.VMEM((states, pad, cats * 64), F32),
            pltpu.VMEM((states, pad, cats * 64), F32),
            pltpu.VMEM((taxa * rows, LANES), F32),
            pltpu.VMEM((taxa * rows, LANES), F32),
            pltpu.VMEM((taxa, rows, LANES), BF16),
            pltpu.VMEM((taxa, rows, 2 * LANES), BF16),
            pltpu.VMEM((taxa - 2, 3 * rows, width), BF16),
            pltpu.VMEM((1, width), F32),
            pltpu.SemaphoreType.DMA((2,)),
        ],
        compiler_params=pltpu.CompilerParams(vmem_limit_bytes=60 * 1024 * 1024),
        name="prune",
    )(
        children,
        site_count,
        slot_gene,
        exchange,
        freqs[None],
        rates[None],
        branch[None],
        tips,
    )
    table = lax.all_to_all(part, ("gene", "site"), split_axis=0, concat_axis=0, tiled=True)
    table = table.reshape(groups, members, 3 * LANES)
    mine = lax.dynamic_index_in_dim(table, lax.axis_index("gene"), 0, keepdims=False)
    mine = jnp.sum(mine, axis=0)
    gene = mine[:GROUP_GENES] / mine[LANES : LANES + GROUP_GENES]
    total = jnp.sum(table[:, :, 2 * LANES]) / (width * members)
    return site, gene[None, :], total


def solution(mesh):
    placed = (
        P("gene", None, None, "site"),
        P(),
        P(),
        P(),
        P(),
        P(),
        P("gene", "site"),
        P("gene", "site"),
    )
    return jax.shard_map(
        on_device,
        mesh=mesh,
        in_specs=placed,
        out_specs=(P("gene", "site"), P("gene", None), P()),
        check_vma=False,
    )
```

```python
import functools

import jax
import jax.numpy as jnp
from jax import lax
from jax.experimental import pallas as pl
from jax.experimental.pallas import tpu as pltpu
from jax.sharding import PartitionSpec as P

GROUP_GENES = 64
TAYLOR = 8
SQUARINGS = 8
LANES = 128
F32 = jnp.float32
BF16 = jnp.bfloat16


def up(value, to):
    return (value + to - 1) // to * to


def kernel(dims, *refs):
    taxa, states, cats, width, slots = dims
    levels = []
    count = taxa // 2
    while count > 1:
        levels.append(pltpu.VMEM((count, 3 * states * cats, width), BF16))
        count //= 2
    rows = states * cats
    half = up(states, 16)
    pl.run_scoped(
        functools.partial(body_of, dims, *refs),
        pltpu.VMEM((taxa, 2 * half, width), BF16),
        pltpu.VMEM((taxa, rows, LANES), BF16),
        pltpu.VMEM((taxa, rows, 2 * LANES), BF16),
        *levels,
    )


def body_of(
    dims,
    children,
    counts,
    genes,
    exchange,
    freqs,
    rates,
    branch,
    tips,
    site_out,
    part_out,
    raw,
    leaf_m,
    leaf_n,
    inner_m,
    inner_n,
    leaf_f,
    inner_f,
    scale,
    sem,
    leaves,
    leaf_p,
    inner_p,
    *levels,
):
    taxa, states, cats, width, slots = dims
    pad = up(states, 8)
    half = up(states, 16)
    rows = states * cats
    chunk = 256
    group = 8
    copy = pltpu.make_async_copy(tips.at[0], raw, sem)
    copy.start()

    row = lax.broadcasted_iota(jnp.int32, (states, states), 0)
    col = lax.broadcasted_iota(jnp.int32, (states, states), 1)
    eye = (row == col).astype(F32)
    sym = (exchange[...] + exchange[...].T) * 0.5 * (1.0 - eye)
    pi = freqs[...] / jnp.sum(freqs[...], axis=1, keepdims=True)
    root = jnp.sqrt(pi)
    root_t = jnp.sqrt(jnp.sum(eye * pi, axis=1, keepdims=True))
    qmat = sym * pi
    qmat = qmat - eye * jnp.sum(qmat, axis=1, keepdims=True)
    rate = -jnp.sum(jnp.sum(qmat * eye * pi, axis=1, keepdims=True), axis=0, keepdims=True)
    qmat = (sym * root * root_t + eye * qmat) / rate
    scaled = rates[...] / jnp.mean(rates[...], axis=1, keepdims=True)
    fill = jnp.zeros((1, 2 * taxa - branch.shape[1]), F32)
    lengths = jnp.concatenate([branch[...], fill], axis=1)
    times = [
        lengths[:, h * taxa : (h + 1) * taxa] * scaled[:, k : k + 1]
        for h in range(2)
        for k in range(cats)
    ]
    times = jnp.concatenate(times, axis=1) / 256.0
    batch = cats * taxa

    powers = [qmat]
    dot = functools.partial(jnp.dot, precision=lax.Precision.HIGHEST, preferred_element_type=F32)
    for order in range(2, TAYLOR + 1):
        lo = order // 2
        powers.append(dot(powers[lo - 1], powers[order - lo - 1]))
    fill = jnp.zeros((pad - states, states), F32)
    powers = [jnp.concatenate([p, fill], axis=0) for p in powers]
    times_b = jnp.broadcast_to(times, (pad, 2 * batch))
    for i in range(states):
        acc = jnp.zeros((pad, 2 * batch), F32)
        for order in range(TAYLOR, 0, -1):
            column = jnp.broadcast_to(powers[order - 1][:, i : i + 1], (pad, 2 * batch))
            acc = (column + acc) * (times_b * (1.0 / order))
        leaf_m[i] = acc[:, :batch]
        inner_m[i] = acc[:, batch:]

    def square(src, dst):
        def part(at, size, after=None):
            two = 2.0 if after is None else 2.0 + 0.0 * after[:1, :batch]
            low = at // 8 * 8
            acc = [src[at + q, low:, :] * two for q in range(size)]
            for j in range(states):
                right = src[j, low:, :]
                for q in range(size):
                    acc[q] = acc[q] + src[at + q, j : j + 1, :] * right
            for q in range(size):
                dst[at + q, low:, :] = acc[q]
                for tile in range(low + 8, pad, 8):
                    real = min(8, states - tile)
                    mirror = acc[q][tile - low : tile - low + real]
                    dst[tile : tile + real, at + q : at + q + 1, :] = mirror[:, None, :]

        pieces = []
        at = 0
        while at < states:
            size = min(2 << (at // 8), 8 - at % 8, states - at)
            pieces.append(functools.partial(part, at, size))
            at += size
        return pieces[::-1]

    target = lax.broadcasted_iota(jnp.int32, (group * half, group * states), 1)
    target = (target & (group - 1)) * half + (target >> 3)
    pick = lax.broadcasted_iota(jnp.int32, (group * half, group * states), 0) == target
    pick = pick.astype(F32).astype(BF16)
    chunks = width // chunk
    rounds = SQUARINGS // 2
    def leaf_step(step, carry):
        for src, dst in ((leaf_m, leaf_n), (leaf_n, leaf_m)):
            for piece in square(src, dst)[::-1]:
                piece()
        return carry

    lax.fori_loop(0, rounds, leaf_step, 0)

    def select(c, carry):
        cols = pl.ds(pl.multiple_of(c * chunk, chunk), chunk)
        for g in range(taxa // group):
            x = raw[:, pl.ds(g * group, group), cols].reshape(states * group, chunk)
            y = jnp.dot(pick, x, preferred_element_type=F32).astype(BF16)
            for one in range(group):
                z = y[one * half : (one + 1) * half]
                leaves[g * group + one, pl.ds(0, half), cols] = z
                leaves[g * group + one, pl.ds(half, half), cols] = z
        return carry

    copy.wait()
    lax.fori_loop(0, chunks, select, 0)

    sub = lax.broadcasted_iota(jnp.int32, (pad, batch), 0)
    root_w = jnp.concatenate([root_t, jnp.ones((pad - states, 1), F32)], axis=0)
    root_w = jnp.broadcast_to(root_w, (pad, batch))
    over = 1.0 / root_w
    across = lax.broadcasted_iota(jnp.int32, (taxa, LANES), 1)
    many = LANES // pad

    def spread(mat, to, turn):
        for start in range(0, states, many):
            size = min(many, states - start)
            tall = []
            for i in range(start, start + size):
                x = mat[i] * (root_w * over[i : i + 1]) + (sub == i).astype(F32)
                tall.append(x)
            tall.append(jnp.zeros((LANES - size * pad, batch), F32))
            z = jnp.concatenate(tall, axis=0).T
            for q in range(size):
                for k in range(cats):
                    at = k * states if turn else 0
                    part = z[k * taxa : (k + 1) * taxa]
                    shift = (at - q * pad) % LANES
                    if shift:
                        part = pltpu.roll(part, shift, 1)
                    part = jnp.where((across >= at) & (across < at + states), part, 0.0)
                    to[pl.ds((k * states + start + q) * (taxa + 1), taxa), :] = part

    spread(leaf_m, leaf_f, False)
    lane = lax.broadcasted_iota(jnp.int32, (rows, LANES), 1)

    unroll = 4

    def split_leaf(step, carry):
        for n in [step * unroll + u for u in range(unroll)]:
            x = leaf_f[pl.ds(n, rows, stride=taxa + 1), :]
            hi = x.astype(BF16).astype(F32)
            leaf_p[n] = (hi + pltpu.roll(x - hi, half, 1)).astype(BF16)
        return carry

    def split_inner(step, carry):
        for n in [step * unroll + u for u in range(unroll)]:
            x = inner_f[pl.ds(n, rows, stride=taxa + 1), :]
            hi = x.astype(BF16).astype(F32)
            turned = pltpu.roll(hi, rows, 1)
            low = pltpu.roll(x - hi, 2 * rows - LANES, 1)
            inner_p[n, :, pl.ds(0, LANES)] = jnp.where(lane < rows, hi, turned).astype(BF16)
            low = jnp.where(lane < 2 * rows - LANES, turned, low)
            inner_p[n, :, pl.ds(LANES, LANES)] = low.astype(BF16)
        return carry

    lax.fori_loop(0, taxa // unroll, split_leaf, 0)

    scale[...] = jnp.zeros_like(scale)

    def store(to, node, cols, p):
        hi = p.astype(BF16)
        lo = (p - hi.astype(F32)).astype(BF16)
        to[node, pl.ds(0, rows), cols] = hi
        to[node, pl.ds(rows, rows), cols] = lo
        to[node, pl.ds(2 * rows, rows), cols] = hi

    def messages(node, level, first):
        ids = [children[side, first + node] for side in range(2)]
        if level == 0:
            mats = [leaf_p[child, :, : 2 * half] for child in ids]
            source, base = leaves, 0
        else:
            mats = [inner_p[child - taxa, :, : 3 * rows] for child in ids]
            source, base = levels[level - 1], taxa + first - 2 * (taxa >> (level + 1))
        for c in range(chunks):
            cols = pl.ds(c * chunk, chunk)
            left, right = (
                jnp.dot(mat, source[child - base, :, cols], preferred_element_type=F32)
                for mat, child in zip(mats, ids)
            )
            yield c, cols, left * right

    def at_nodes(step, carry, level, first, each):
        parts, done = [], 0
        if level == 0:
            parts = square(inner_m, inner_n)
            parts = square(inner_n, inner_m) + parts
            total = len(parts)
            every = each * chunks / total
            parts.pop()()
        for u in range(each):
            node = step * each + u
            for c, cols, p in messages(node, level, first):
                if level % 3 == 2:
                    top = jnp.max(p, axis=0, keepdims=True)
                    p = p * (1.0 / top)
                    scale[:, cols] = scale[:, cols] + jnp.log(top)
                store(levels[level], node, cols, p)
                done += 1
                while parts and done >= every * (total - len(parts)):
                    parts.pop()(p)
        return carry

    first, count, level = 0, taxa // 2, 0
    assert count % rounds == 0
    while count > 1:
        each = 2 if level else count // rounds
        lax.fori_loop(
            0, count // each, functools.partial(at_nodes, level=level, first=first, each=each), 0
        )
        if level == 0:
            spread(inner_m, inner_f, True)
            lax.fori_loop(0, taxa // unroll, split_inner, 0)
        first, count, level = first + count, count // 2, level + 1

    wide = lax.broadcasted_iota(jnp.int32, (rows, states), 0)
    tall = lax.broadcasted_iota(jnp.int32, (rows, states), 1)
    weight = jnp.where(wide % states == tall, pi, 0.0)
    weight = jnp.sum(weight, axis=1, keepdims=True) / cats
    line = lax.broadcasted_iota(jnp.int32, (1, LANES), 1)
    tile = width // slots
    sums = jnp.zeros((1, LANES), F32)
    sizes = jnp.zeros((1, LANES), F32)
    whole = jnp.zeros((1, 1), F32)
    for c, cols, p in messages(0, level, first):
        lik = jnp.sum(p * weight, axis=0, keepdims=True)
        value = jnp.log(lik) + scale[:, cols]
        for t in range(chunk // tile):
            slot = c * (chunk // tile) + t
            size = counts[0, slot]
            part = jnp.where(line < size, value[:, t * tile : (t + 1) * tile], 0.0)
            site_out[:, pl.ds(slot * tile, tile)] = part
            sum_of = jnp.sum(part, axis=1, keepdims=True)
            hit = (line == genes[0, slot]) & (size > 0)
            sums = sums + jnp.where(hit, sum_of, 0.0)
            sizes = sizes + jnp.where(hit, size.astype(F32), 0.0)
            whole = whole + sum_of
    tail = jnp.where(line == 0, whole, 0.0)
    message_row = jnp.concatenate([sums, sizes, tail], axis=1)
    part_out[...] = jnp.broadcast_to(message_row[None], part_out.shape)


def on_device(tips, exchange, freqs, rates, branch, children, slot_gene, site_count):
    taxa, states, width = tips.shape[1:]
    slots = site_count.shape[1]
    cats = rates.shape[0]
    rows = states * cats
    members = lax.axis_size("site")
    groups = lax.axis_size("gene")
    devices = members * groups
    pad = up(states, 8)
    smem = pl.BlockSpec(memory_space=pltpu.SMEM)
    vmem = pl.BlockSpec(memory_space=pltpu.VMEM)
    levels = []
    count = taxa // 2
    while count > 1:
        levels.append(pltpu.VMEM((count, 3 * rows, width), BF16))
        count //= 2
    site, part = pl.pallas_call(
        functools.partial(kernel, (taxa, states, cats, width, slots)),
        out_shape=(
            jax.ShapeDtypeStruct((1, width), F32),
            jax.ShapeDtypeStruct((devices, 1, 3 * LANES), F32),
        ),
        in_specs=[smem] * 3 + [vmem] * 4 + [pl.BlockSpec(memory_space=pl.ANY)],
        out_specs=(vmem, vmem),
        scratch_shapes=[
            pltpu.VMEM((states, taxa, width), BF16),
            pltpu.VMEM((states, pad, cats * taxa), F32),
            pltpu.VMEM((states, pad, cats * taxa), F32),
            pltpu.VMEM((states, pad, cats * taxa), F32),
            pltpu.VMEM((states, pad, cats * taxa), F32),
            pltpu.VMEM(((taxa + 1) * rows, LANES), F32),
            pltpu.VMEM(((taxa + 1) * rows, LANES), F32),
            pltpu.VMEM((1, width), F32),
            pltpu.SemaphoreType.DMA,
        ],
        compiler_params=pltpu.CompilerParams(vmem_limit_bytes=60 * 1024 * 1024),
        name="prune",
    )(
        children.T,
        site_count,
        slot_gene,
        exchange,
        freqs[None],
        rates[None],
        branch[None],
        tips.transpose(0, 2, 1, 3),
    )
    table = lax.all_to_all(part, ("gene", "site"), split_axis=0, concat_axis=0, tiled=True)
    table = table.reshape(groups, members, 3 * LANES)
    mine = lax.dynamic_index_in_dim(table, lax.axis_index("gene"), 0, keepdims=False)
    mine = jnp.sum(mine, axis=0)
    gene = mine[:GROUP_GENES] / mine[LANES : LANES + GROUP_GENES]
    total = jnp.sum(table[:, :, 2 * LANES]) / (width * members)
    return site, gene[None, :], total


def solution(mesh):
    placed = (
        P("gene", None, None, "site"),
        P(),
        P(),
        P(),
        P(),
        P(),
        P("gene", "site"),
        P("gene", "site"),
    )
    return jax.shard_map(
        on_device,
        mesh=mesh,
        in_specs=placed,
        out_specs=(P("gene", "site"), P("gene", None), P()),
        check_vma=False,
    )
```

```python
import functools

import jax
import jax.numpy as jnp
from jax import lax
from jax.experimental import pallas as pl
from jax.experimental.pallas import tpu as pltpu
from jax.sharding import PartitionSpec as P

GROUP_GENES = 64
TAYLOR = 8
SQUARINGS = 8
LANES = 128
F32 = jnp.float32
BF16 = jnp.bfloat16


def up(value, to):
    return (value + to - 1) // to * to


def kernel(dims, *refs):
    taxa, states, cats, width, slots = dims
    levels = []
    count = taxa // 2
    while count > 1:
        levels.append(pltpu.VMEM((count, 2 * states * cats, width), BF16))
        count //= 2
    rows = states * cats
    half = up(states, 16)
    pl.run_scoped(
        functools.partial(body_of, dims, *refs),
        pltpu.VMEM((taxa, 2 * half, width), BF16),
        pltpu.VMEM((taxa, rows, LANES), BF16),
        pltpu.VMEM((taxa, 2 * rows, 2 * LANES), BF16),
        *levels,
    )


def body_of(
    dims,
    children,
    counts,
    genes,
    exchange,
    freqs,
    rates,
    branch,
    tips,
    site_out,
    part_out,
    raw,
    leaf_m,
    leaf_n,
    inner_m,
    inner_n,
    leaf_f,
    inner_f,
    scale,
    sem,
    leaves,
    leaf_p,
    inner_p,
    *levels,
):
    taxa, states, cats, width, slots = dims
    pad = up(states, 8)
    half = up(states, 16)
    rows = states * cats
    chunk = 256
    group = 8
    copy = pltpu.make_async_copy(tips.at[0], raw, sem)
    copy.start()

    row = lax.broadcasted_iota(jnp.int32, (states, states), 0)
    col = lax.broadcasted_iota(jnp.int32, (states, states), 1)
    eye = (row == col).astype(F32)
    sym = (exchange[...] + exchange[...].T) * 0.5 * (1.0 - eye)
    pi = freqs[...] / jnp.sum(freqs[...], axis=1, keepdims=True)
    root = jnp.sqrt(pi)
    root_t = jnp.sqrt(jnp.sum(eye * pi, axis=1, keepdims=True))
    qmat = sym * pi
    qmat = qmat - eye * jnp.sum(qmat, axis=1, keepdims=True)
    rate = -jnp.sum(jnp.sum(qmat * eye * pi, axis=1, keepdims=True), axis=0, keepdims=True)
    qmat = (sym * root * root_t + eye * qmat) / rate
    scaled = rates[...] / jnp.mean(rates[...], axis=1, keepdims=True)
    fill = jnp.zeros((1, 2 * taxa - branch.shape[1]), F32)
    lengths = jnp.concatenate([branch[...], fill], axis=1)
    times = [
        lengths[:, h * taxa : (h + 1) * taxa] * scaled[:, k : k + 1]
        for h in range(2)
        for k in range(cats)
    ]
    times = jnp.concatenate(times, axis=1) / 256.0
    batch = cats * taxa

    powers = [qmat]
    dot = functools.partial(jnp.dot, precision=lax.Precision.HIGHEST, preferred_element_type=F32)
    for order in range(2, TAYLOR + 1):
        lo = order // 2
        powers.append(dot(powers[lo - 1], powers[order - lo - 1]))
    fill = jnp.zeros((pad - states, states), F32)
    powers = [jnp.concatenate([p, fill], axis=0) for p in powers]
    times_b = jnp.broadcast_to(times, (pad, 2 * batch))
    for i in range(states):
        acc = jnp.zeros((pad, 2 * batch), F32)
        for order in range(TAYLOR, 0, -1):
            column = jnp.broadcast_to(powers[order - 1][:, i : i + 1], (pad, 2 * batch))
            acc = (column + acc) * (times_b * (1.0 / order))
        leaf_m[i] = acc[:, :batch]
        inner_m[i] = acc[:, batch:]

    def square(src, dst):
        def part(at, size):
            low = at // 8 * 8
            acc = [src[at + q, low:, :] * 2.0 for q in range(size)]
            for j in range(states):
                right = src[j, low:, :]
                for q in range(size):
                    acc[q] = acc[q] + src[at + q, j : j + 1, :] * right
            for q in range(size):
                dst[at + q, low:, :] = acc[q]
                for tile in range(low + 8, pad, 8):
                    real = min(8, states - tile)
                    mirror = acc[q][tile - low : tile - low + real]
                    dst[tile : tile + real, at + q : at + q + 1, :] = mirror[:, None, :]

        pieces = []
        at = 0
        while at < states:
            size = min(4 << (at // 8), 8 - at % 8, states - at)
            pieces.append(functools.partial(part, at, size))
            at += size
        return pieces[::-1]

    target = lax.broadcasted_iota(jnp.int32, (group * half, group * states), 1)
    target = (target & (group - 1)) * half + (target >> 3)
    pick = lax.broadcasted_iota(jnp.int32, (group * half, group * states), 0) == target
    pick = pick.astype(F32).astype(BF16)
    chunks = width // chunk
    rounds = SQUARINGS // 2
    groups = taxa // group

    def select(c, g):
        cols = pl.ds(pl.multiple_of(c * chunk, chunk), chunk)
        x = raw[:, pl.ds(g * group, group), cols].reshape(states * group, chunk)
        y = jnp.dot(pick, x, preferred_element_type=F32)
        z = y.astype(BF16)
        for one in range(group):
            part = z[one * half : (one + 1) * half]
            leaves[g * group + one, pl.ds(0, half), cols] = part
            leaves[g * group + one, pl.ds(half, half), cols] = part

    def leaf_step(step, carry, beside):
        parts = square(leaf_n, leaf_m) + square(leaf_m, leaf_n)
        total = len(parts)
        work = [(c, g) for c in range(beside) for g in range(groups)]
        if not work:
            while parts:
                parts.pop()()
        else:
            parts.pop()()
        for done, (c, g) in enumerate(work):
            select(step * beside + c, g)
            while parts and (done + 1) * total >= len(work) * (total - len(parts)):
                parts.pop()()
        return carry

    early = rounds // 2
    lax.fori_loop(0, early, functools.partial(leaf_step, beside=0), 0)
    copy.wait()
    late = rounds - early
    lax.fori_loop(0, late, functools.partial(leaf_step, beside=chunks // late), 0)

    sub = lax.broadcasted_iota(jnp.int32, (pad, batch), 0)
    root_w = jnp.concatenate([root_t, jnp.ones((pad - states, 1), F32)], axis=0)
    root_w = jnp.broadcast_to(root_w, (pad, batch))
    over = 1.0 / root_w
    across = lax.broadcasted_iota(jnp.int32, (taxa, LANES), 1)
    many = LANES // pad

    def spread(mat, to, turn):
        for start in range(0, states, many):
            size = min(many, states - start)
            tall = []
            for i in range(start, start + size):
                x = mat[i] * (root_w * over[i : i + 1]) + (sub == i).astype(F32)
                tall.append(x)
            tall.append(jnp.zeros((LANES - size * pad, batch), F32))
            z = jnp.concatenate(tall, axis=0).T
            for q in range(size):
                for k in range(cats):
                    at = k * states if turn else 0
                    part = z[k * taxa : (k + 1) * taxa]
                    shift = (at - q * pad) % LANES
                    if shift:
                        part = pltpu.roll(part, shift, 1)
                    part = jnp.where((across >= at) & (across < at + states), part, 0.0)
                    to[pl.ds((k * states + start + q) * (taxa + 1), taxa), :] = part

    spread(leaf_m, leaf_f, False)
    lane = lax.broadcasted_iota(jnp.int32, (rows, LANES), 1)

    unroll = 4

    def split_leaf(step, carry):
        for n in [step * unroll + u for u in range(unroll)]:
            x = leaf_f[pl.ds(n, rows, stride=taxa + 1), :]
            hi = x.astype(BF16).astype(F32)
            leaf_p[n] = (hi + pltpu.roll(x - hi, half, 1)).astype(BF16)
        return carry

    def split_inner(step, carry):
        for n in [step * unroll + u for u in range(unroll)]:
            x = inner_f[pl.ds(n, rows, stride=taxa + 1), :]
            hi = x.astype(BF16).astype(F32)
            turned = pltpu.roll(hi, rows, 1)
            inner_p[n, :rows, :LANES] = jnp.where(lane < rows, hi, turned).astype(BF16)
            inner_p[n, :rows, LANES:] = jnp.where(lane < 2 * rows - LANES, turned, 0.0).astype(BF16)
            inner_p[n, rows:, :LANES] = (x - hi).astype(BF16)
            inner_p[n, rows:, LANES:] = jnp.zeros((rows, LANES), BF16)
        return carry

    lax.fori_loop(0, taxa // unroll, split_leaf, 0)

    scale[...] = jnp.zeros_like(scale)

    def store(to, node, cols, p):
        hi = p.astype(BF16)
        lo = (p - hi.astype(F32)).astype(BF16)
        to[node, pl.ds(0, rows), cols] = hi
        to[node, pl.ds(rows, rows), cols] = lo

    def messages(node, level, first):
        ids = [children[side, first + node] for side in range(2)]
        if level == 0:
            mats = [leaf_p[child, :, : 2 * half] for child in ids]
            source, base = leaves, 0
        else:
            mats = [inner_p[child - taxa, :, : 2 * rows] for child in ids]
            source, base = levels[level - 1], taxa + first - 2 * (taxa >> (level + 1))
        for c in range(chunks):
            cols = pl.ds(c * chunk, chunk)
            left, right = (
                jnp.dot(mat, source[child - base, :, cols], preferred_element_type=F32)
                for mat, child in zip(mats, ids)
            )
            if level:
                left, right = (side[:rows] + side[rows:] for side in (left, right))
            yield c, cols, left * right

    def at_nodes(step, carry, level, first, each):
        parts, done = [], 0
        if level == 0:
            parts = square(inner_m, inner_n)
            parts = square(inner_n, inner_m) + parts
            total = len(parts)
            every = each * chunks / total
            parts.pop()()
        for u in range(each):
            node = step * each + u
            for c, cols, p in messages(node, level, first):
                if level % 3 == 2:
                    top = jnp.max(p, axis=0, keepdims=True)
                    p = p * (1.0 / top)
                    scale[:, cols] = scale[:, cols] + jnp.log(top)
                store(levels[level], node, cols, p)
                done += 1
                while parts and done >= every * (total - len(parts)):
                    parts.pop()()
        return carry

    first, count, level = 0, taxa // 2, 0
    assert count % rounds == 0
    while count > 1:
        each = 2 if level else count // rounds
        lax.fori_loop(
            0, count // each, functools.partial(at_nodes, level=level, first=first, each=each), 0
        )
        if level == 0:
            spread(inner_m, inner_f, True)
            lax.fori_loop(0, taxa // unroll, split_inner, 0)
        first, count, level = first + count, count // 2, level + 1

    wide = lax.broadcasted_iota(jnp.int32, (rows, states), 0)
    tall = lax.broadcasted_iota(jnp.int32, (rows, states), 1)
    weight = jnp.where(wide % states == tall, pi, 0.0)
    weight = jnp.sum(weight, axis=1, keepdims=True) / cats
    line = lax.broadcasted_iota(jnp.int32, (1, LANES), 1)
    tile = width // slots
    sums = jnp.zeros((1, LANES), F32)
    sizes = jnp.zeros((1, LANES), F32)
    whole = jnp.zeros((1, 1), F32)
    for c, cols, p in messages(0, level, first):
        lik = jnp.sum(p * weight, axis=0, keepdims=True)
        value = jnp.log(lik) + scale[:, cols]
        for t in range(chunk // tile):
            slot = c * (chunk // tile) + t
            size = counts[0, slot]
            part = jnp.where(line < size, value[:, t * tile : (t + 1) * tile], 0.0)
            site_out[:, pl.ds(slot * tile, tile)] = part
            sum_of = jnp.sum(part, axis=1, keepdims=True)
            hit = (line == genes[0, slot]) & (size > 0)
            sums = sums + jnp.where(hit, sum_of, 0.0)
            sizes = sizes + jnp.where(hit, size.astype(F32), 0.0)
            whole = whole + sum_of
    tail = jnp.where(line == 0, whole, 0.0)
    message_row = jnp.concatenate([sums, sizes, tail], axis=1)
    part_out[...] = jnp.broadcast_to(message_row[None], part_out.shape)


def on_device(tips, exchange, freqs, rates, branch, children, slot_gene, site_count):
    taxa, states, width = tips.shape[1:]
    slots = site_count.shape[1]
    cats = rates.shape[0]
    rows = states * cats
    members = lax.axis_size("site")
    groups = lax.axis_size("gene")
    devices = members * groups
    pad = up(states, 8)
    smem = pl.BlockSpec(memory_space=pltpu.SMEM)
    vmem = pl.BlockSpec(memory_space=pltpu.VMEM)
    levels = []
    count = taxa // 2
    while count > 1:
        levels.append(pltpu.VMEM((count, 3 * rows, width), BF16))
        count //= 2
    site, part = pl.pallas_call(
        functools.partial(kernel, (taxa, states, cats, width, slots)),
        out_shape=(
            jax.ShapeDtypeStruct((1, width), F32),
            jax.ShapeDtypeStruct((devices, 1, 3 * LANES), F32),
        ),
        in_specs=[smem] * 3 + [vmem] * 4 + [pl.BlockSpec(memory_space=pl.ANY)],
        out_specs=(vmem, vmem),
        scratch_shapes=[
            pltpu.VMEM((states, taxa, width), BF16),
            pltpu.VMEM((states, pad, cats * taxa), F32),
            pltpu.VMEM((states, pad, cats * taxa), F32),
            pltpu.VMEM((states, pad, cats * taxa), F32),
            pltpu.VMEM((states, pad, cats * taxa), F32),
            pltpu.VMEM(((taxa + 1) * rows, LANES), F32),
            pltpu.VMEM(((taxa + 1) * rows, LANES), F32),
            pltpu.VMEM((1, width), F32),
            pltpu.SemaphoreType.DMA,
        ],
        compiler_params=pltpu.CompilerParams(vmem_limit_bytes=60 * 1024 * 1024),
        name="prune",
    )(
        children.T,
        site_count,
        slot_gene,
        exchange,
        freqs[None],
        rates[None],
        branch[None],
        tips.transpose(0, 2, 1, 3),
    )
    table = lax.all_to_all(part, ("gene", "site"), split_axis=0, concat_axis=0, tiled=True)
    table = table.reshape(groups, members, 3 * LANES)
    mine = lax.dynamic_index_in_dim(table, lax.axis_index("gene"), 0, keepdims=False)
    mine = jnp.sum(mine, axis=0)
    gene = mine[:GROUP_GENES] / mine[LANES : LANES + GROUP_GENES]
    total = jnp.sum(table[:, :, 2 * LANES]) / (width * members)
    return site, gene[None, :], total


def solution(mesh):
    placed = (
        P("gene", None, None, "site"),
        P(),
        P(),
        P(),
        P(),
        P(),
        P("gene", "site"),
        P("gene", "site"),
    )
    return jax.shard_map(
        on_device,
        mesh=mesh,
        in_specs=placed,
        out_specs=(P("gene", "site"), P("gene", None), P()),
        check_vma=False,
    )
```

```python
import functools

import jax
import jax.numpy as jnp
from jax import lax
from jax.experimental import pallas as pl
from jax.experimental.pallas import tpu as pltpu
from jax.sharding import PartitionSpec as P

GROUP_GENES = 64
TAYLOR = 8
SQUARINGS = 8
LANES = 128
F32 = jnp.float32
BF16 = jnp.bfloat16


def up(value, to):
    return (value + to - 1) // to * to


def kernel(dims, *refs):
    taxa, states, cats, width, slots = dims
    levels = []
    count = taxa // 2
    while count > 1:
        levels.append(pltpu.VMEM((count, 2 * states * cats, width), BF16))
        count //= 2
    rows = states * cats
    half = up(states, 16)
    pl.run_scoped(
        functools.partial(body_of, dims, *refs),
        pltpu.VMEM((taxa, 2 * half, width), BF16),
        pltpu.VMEM((taxa, rows, LANES), BF16),
        pltpu.VMEM((8 * half, 8 * states), BF16),
        pltpu.VMEM((taxa, 2 * rows, 2 * LANES), BF16),
        *levels,
    )


def body_of(
    dims,
    children,
    counts,
    genes,
    exchange,
    freqs,
    rates,
    branch,
    tips,
    site_out,
    part_out,
    raw,
    leaf_m,
    leaf_n,
    inner_m,
    inner_n,
    leaf_f,
    inner_f,
    scale,
    sem,
    leaves,
    leaf_p,
    picks,
    inner_p,
    *levels,
):
    taxa, states, cats, width, slots = dims
    pad = up(states, 8)
    half = up(states, 16)
    rows = states * cats
    chunk = 256
    group = 8
    copy = pltpu.make_async_copy(tips.at[0], raw, sem)
    copy.start()

    row = lax.broadcasted_iota(jnp.int32, (states, states), 0)
    col = lax.broadcasted_iota(jnp.int32, (states, states), 1)
    eye = (row == col).astype(F32)
    sym = (exchange[...] + exchange[...].T) * 0.5 * (1.0 - eye)
    pi = freqs[...] / jnp.sum(freqs[...], axis=1, keepdims=True)
    root = jnp.sqrt(pi)
    root_t = jnp.sqrt(jnp.sum(eye * pi, axis=1, keepdims=True))
    qmat = sym * pi
    qmat = qmat - eye * jnp.sum(qmat, axis=1, keepdims=True)
    rate = -jnp.sum(jnp.sum(qmat * eye * pi, axis=1, keepdims=True), axis=0, keepdims=True)
    qmat = (sym * root * root_t + eye * qmat) / rate
    scaled = rates[...] / jnp.mean(rates[...], axis=1, keepdims=True)
    fill = jnp.zeros((1, 2 * taxa - branch.shape[1]), F32)
    lengths = jnp.concatenate([branch[...], fill], axis=1)
    times = [
        lengths[:, h * taxa : (h + 1) * taxa] * scaled[:, k : k + 1]
        for h in range(2)
        for k in range(cats)
    ]
    times = jnp.concatenate(times, axis=1) / 256.0
    batch = cats * taxa

    powers = [qmat]
    dot = functools.partial(jnp.dot, precision=lax.Precision.HIGHEST, preferred_element_type=F32)
    for order in range(2, TAYLOR + 1):
        lo = order // 2
        powers.append(dot(powers[lo - 1], powers[order - lo - 1]))
    fill = jnp.zeros((pad - states, states), F32)
    powers = [jnp.concatenate([p, fill], axis=0) for p in powers]
    def put(dst, i, low, value):
        dst[i, low:, :] = value
        for tile in range(low + 8, pad, 8):
            real = min(8, states - tile)
            mirror = value[tile - low : tile - low + real]
            dst[tile : tile + real, i : i + 1, :] = mirror[:, None, :]

    for i in range(states):
        low = i // 8 * 8
        times_b = jnp.broadcast_to(times, (pad - low, 2 * batch))
        acc = jnp.zeros((pad - low, 2 * batch), F32)
        for order in range(TAYLOR, 0, -1):
            column = jnp.broadcast_to(powers[order - 1][low:, i : i + 1], acc.shape)
            acc = (column + acc) * (times_b * (1.0 / order))
        put(leaf_m, i, low, acc[:, :batch])
        put(inner_m, i, low, acc[:, batch:])

    def square(src, dst, most):
        def part(at, size):
            low = at // 8 * 8
            acc = [src[at + q, low:, :] * 2.0 for q in range(size)]
            for j in range(states):
                right = src[j, low:, :]
                for q in range(size):
                    acc[q] = acc[q] + src[at + q, j : j + 1, :] * right
            for q in range(size):
                put(dst, at + q, low, acc[q])

        pieces = []
        at = 0
        while at < states:
            size = min(most, 8 - at % 8, states - at)
            pieces.append(functools.partial(part, at, size))
            at += size
        return pieces[::-1]

    target = lax.broadcasted_iota(jnp.int32, (group * half, group * states), 1)
    target = (target & (group - 1)) * half + (target >> 3)
    pick = lax.broadcasted_iota(jnp.int32, (group * half, group * states), 0) == target
    picks[...] = pick.astype(F32).astype(BF16)
    chunks = width // chunk
    rounds = SQUARINGS // 2
    groups = taxa // group

    def select(c, g):
        cols = pl.ds(pl.multiple_of(c * chunk, chunk), chunk)
        x = raw[:, pl.ds(g * group, group), cols].reshape(states * group, chunk)
        y = jnp.dot(picks[...], x, preferred_element_type=F32)
        z = y.astype(BF16)
        for one in range(group):
            part = z[one * half : (one + 1) * half]
            leaves[g * group + one, pl.ds(0, half), cols] = part
            leaves[g * group + one, pl.ds(half, half), cols] = part

    def leaf_step(step, carry, beside):
        parts = square(leaf_n, leaf_m, 8) + square(leaf_m, leaf_n, 8)
        total = len(parts)
        work = [(c, g) for c in range(beside) for g in range(groups)]
        if not work:
            while parts:
                parts.pop()()
        else:
            parts.pop()()
        for done, (c, g) in enumerate(work):
            select(step * beside + c, g)
            while parts and (done + 1) * total >= len(work) * (total - len(parts)):
                parts.pop()()
        return carry

    early = rounds // 2
    lax.fori_loop(0, early, functools.partial(leaf_step, beside=0), 0)
    copy.wait()
    late = rounds - early
    lax.fori_loop(0, late, functools.partial(leaf_step, beside=chunks // late), 0)

    sub = lax.broadcasted_iota(jnp.int32, (pad, batch), 0)
    root_w = jnp.concatenate([root_t, jnp.ones((pad - states, 1), F32)], axis=0)
    root_w = jnp.broadcast_to(root_w, (pad, batch))
    over = 1.0 / root_w
    across = lax.broadcasted_iota(jnp.int32, (taxa, LANES), 1)
    many = LANES // pad

    def spread(mat, to, turn):
        for start in range(0, states, many):
            size = min(many, states - start)
            tall = []
            for i in range(start, start + size):
                x = mat[i] * (root_w * over[i : i + 1]) + (sub == i).astype(F32)
                tall.append(x)
            tall.append(jnp.zeros((LANES - size * pad, batch), F32))
            z = jnp.concatenate(tall, axis=0).T
            for q in range(size):
                for k in range(cats):
                    at = k * states if turn else 0
                    part = z[k * taxa : (k + 1) * taxa]
                    shift = (at - q * pad) % LANES
                    if shift:
                        part = pltpu.roll(part, shift, 1)
                    part = jnp.where((across >= at) & (across < at + states), part, 0.0)
                    to[pl.ds((k * states + start + q) * (taxa + 1), taxa), :] = part

    spread(leaf_m, leaf_f, False)
    lane = lax.broadcasted_iota(jnp.int32, (rows, LANES), 1)

    unroll = 4

    def split_leaf(step, carry):
        for n in [step * unroll + u for u in range(unroll)]:
            x = leaf_f[pl.ds(n, rows, stride=taxa + 1), :]
            hi = x.astype(BF16).astype(F32)
            leaf_p[n] = (hi + pltpu.roll(x - hi, half, 1)).astype(BF16)
        return carry

    def split_inner(step, carry):
        for n in [step * unroll + u for u in range(unroll)]:
            x = inner_f[pl.ds(n, rows, stride=taxa + 1), :]
            hi = x.astype(BF16).astype(F32)
            turned = pltpu.roll(hi, rows, 1)
            inner_p[n, :rows, :LANES] = jnp.where(lane < rows, hi, turned).astype(BF16)
            inner_p[n, :rows, LANES:] = jnp.where(lane < 2 * rows - LANES, turned, 0.0).astype(BF16)
            inner_p[n, rows:, :LANES] = (x - hi).astype(BF16)
            inner_p[n, rows:, LANES:] = jnp.zeros((rows, LANES), BF16)
        return carry

    lax.fori_loop(0, taxa // unroll, split_leaf, 0)

    scale[...] = jnp.zeros_like(scale)

    def store(to, node, cols, p):
        hi = p.astype(BF16)
        lo = (p - hi.astype(F32)).astype(BF16)
        to[node, pl.ds(0, rows), cols] = hi
        to[node, pl.ds(rows, rows), cols] = lo

    def messages(node, level, first):
        ids = [children[side, first + node] for side in range(2)]
        if level == 0:
            mats = [leaf_p[child, :, : 2 * half] for child in ids]
            source, base = leaves, 0
        else:
            mats = [inner_p[child - taxa, :, : 2 * rows] for child in ids]
            source, base = levels[level - 1], taxa + first - 2 * (taxa >> (level + 1))
        for c in range(chunks):
            cols = pl.ds(c * chunk, chunk)
            left, right = (
                jnp.dot(mat, source[child - base, :, cols], preferred_element_type=F32)
                for mat, child in zip(mats, ids)
            )
            if level:
                left, right = (side[:rows] + side[rows:] for side in (left, right))
            yield c, cols, left * right

    def at_nodes(step, carry, level, first, each):
        parts, done = [], 0
        if level == 0:
            parts = square(inner_m, inner_n, 8)
            parts = square(inner_n, inner_m, 2) + parts
            total = len(parts)
            every = each * chunks / total
            parts.pop()()
        for u in range(each):
            node = step * each + u
            for c, cols, p in messages(node, level, first):
                if level % 3 == 2:
                    top = jnp.max(p, axis=0, keepdims=True)
                    p = p * (1.0 / top)
                    scale[:, cols] = scale[:, cols] + jnp.log(top)
                store(levels[level], node, cols, p)
                done += 1
                while parts and done >= every * (total - len(parts)):
                    parts.pop()()
        return carry

    first, count, level = 0, taxa // 2, 0
    assert count % rounds == 0
    while count > 1:
        each = min(4, count) if level else count // rounds
        lax.fori_loop(
            0, count // each, functools.partial(at_nodes, level=level, first=first, each=each), 0
        )
        if level == 0:
            spread(inner_m, inner_f, True)
            lax.fori_loop(0, taxa // unroll, split_inner, 0)
        first, count, level = first + count, count // 2, level + 1

    wide = lax.broadcasted_iota(jnp.int32, (rows, states), 0)
    tall = lax.broadcasted_iota(jnp.int32, (rows, states), 1)
    weight = jnp.where(wide % states == tall, pi, 0.0)
    weight = jnp.sum(weight, axis=1, keepdims=True) / cats
    line = lax.broadcasted_iota(jnp.int32, (1, LANES), 1)
    tile = width // slots
    sums = jnp.zeros((1, LANES), F32)
    for c, cols, p in messages(0, level, first):
        lik = jnp.sum(p * weight, axis=0, keepdims=True)
        value = jnp.log(lik) + scale[:, cols]
        for t in range(chunk // tile):
            slot = c * (chunk // tile) + t
            size = counts[0, slot]
            part = jnp.where(line < size, value[:, t * tile : (t + 1) * tile], 0.0)
            site_out[:, pl.ds(slot * tile, tile)] = part
            sum_of = jnp.sum(part, axis=1, keepdims=True)
            gene = jnp.where(size > 0, genes[0, slot], 2 * GROUP_GENES)
            sums = sums + jnp.where(line == gene, sum_of, 0.0)
            sums = sums + jnp.where(line == gene + GROUP_GENES, size.astype(F32), 0.0)
    part_out[...] = jnp.broadcast_to(sums[None], part_out.shape)


def on_device(tips, exchange, freqs, rates, branch, children, slot_gene, site_count):
    taxa, states, width = tips.shape[1:]
    slots = site_count.shape[1]
    cats = rates.shape[0]
    rows = states * cats
    members = lax.axis_size("site")
    groups = lax.axis_size("gene")
    devices = members * groups
    pad = up(states, 8)
    smem = pl.BlockSpec(memory_space=pltpu.SMEM)
    vmem = pl.BlockSpec(memory_space=pltpu.VMEM)
    levels = []
    count = taxa // 2
    while count > 1:
        levels.append(pltpu.VMEM((count, 3 * rows, width), BF16))
        count //= 2
    site, part = pl.pallas_call(
        functools.partial(kernel, (taxa, states, cats, width, slots)),
        out_shape=(
            jax.ShapeDtypeStruct((1, width), F32),
            jax.ShapeDtypeStruct((devices, 1, 2 * GROUP_GENES), F32),
        ),
        in_specs=[smem] * 3 + [vmem] * 4 + [pl.BlockSpec(memory_space=pl.ANY)],
        out_specs=(vmem, vmem),
        scratch_shapes=[
            pltpu.VMEM((states, taxa, width), BF16),
            pltpu.VMEM((states, pad, cats * taxa), F32),
            pltpu.VMEM((states, pad, cats * taxa), F32),
            pltpu.VMEM((states, pad, cats * taxa), F32),
            pltpu.VMEM((states, pad, cats * taxa), F32),
            pltpu.VMEM(((taxa + 1) * rows, LANES), F32),
            pltpu.VMEM(((taxa + 1) * rows, LANES), F32),
            pltpu.VMEM((1, width), F32),
            pltpu.SemaphoreType.DMA,
        ],
        compiler_params=pltpu.CompilerParams(vmem_limit_bytes=60 * 1024 * 1024),
        name="prune",
    )(
        children.T,
        site_count,
        slot_gene,
        exchange,
        freqs[None],
        rates[None],
        branch[None],
        tips.transpose(0, 2, 1, 3),
    )
    table = lax.all_to_all(part, ("gene", "site"), split_axis=0, concat_axis=0, tiled=True)
    table = table.reshape(groups, members, 2 * GROUP_GENES)
    mine = lax.dynamic_index_in_dim(table, lax.axis_index("gene"), 0, keepdims=False)
    mine = jnp.sum(mine, axis=0)
    gene = mine[:GROUP_GENES] / mine[GROUP_GENES:]
    total = jnp.sum(table[:, :, :GROUP_GENES]) / (width * members)
    return site, gene[None, :], total


def solution(mesh):
    placed = (
        P("gene", None, None, "site"),
        P(),
        P(),
        P(),
        P(),
        P(),
        P("gene", "site"),
        P("gene", "site"),
    )
    return jax.shard_map(
        on_device,
        mesh=mesh,
        in_specs=placed,
        out_specs=(P("gene", "site"), P("gene", None), P()),
        check_vma=False,
    )
```

```python
import functools

import jax
import jax.numpy as jnp
from jax import lax
from jax.experimental import pallas as pl
from jax.experimental.pallas import tpu as pltpu
from jax.sharding import PartitionSpec as P

GROUP_GENES = 64
TAYLOR = 8
SQUARINGS = 8
LANES = 128
F32 = jnp.float32
BF16 = jnp.bfloat16


def up(value, to):
    return (value + to - 1) // to * to


def kernel(dims, *refs):
    taxa, states, cats, width, slots = dims
    levels = []
    count = taxa // 2
    while count > 1:
        levels.append(pltpu.VMEM((count, 2 * states * cats, width), BF16))
        count //= 2
    rows = states * cats
    half = up(states, 16)
    pl.run_scoped(
        functools.partial(body_of, dims, *refs),
        pltpu.VMEM((taxa, 2 * half, width), BF16),
        pltpu.VMEM((taxa, rows, LANES), BF16),
        pltpu.VMEM((8 * half, 8 * states), BF16),
        pltpu.VMEM((taxa, 2 * rows, 2 * LANES), BF16),
        *levels,
    )


def body_of(
    dims,
    children,
    counts,
    genes,
    exchange,
    freqs,
    rates,
    branch,
    tips,
    site_out,
    part_out,
    raw,
    leaf_m,
    leaf_n,
    inner_m,
    inner_n,
    leaf_f,
    inner_f,
    scale,
    sem,
    leaves,
    leaf_p,
    picks,
    inner_p,
    *levels,
):
    taxa, states, cats, width, slots = dims
    pad = up(states, 8)
    half = up(states, 16)
    rows = states * cats
    chunk = 256
    group = 8
    copy = pltpu.make_async_copy(tips.at[0], raw, sem)
    copy.start()

    row = lax.broadcasted_iota(jnp.int32, (states, states), 0)
    col = lax.broadcasted_iota(jnp.int32, (states, states), 1)
    eye = (row == col).astype(F32)
    sym = (exchange[...] + exchange[...].T) * 0.5 * (1.0 - eye)
    pi = freqs[...] / jnp.sum(freqs[...], axis=1, keepdims=True)
    root = jnp.sqrt(pi)
    root_t = jnp.sqrt(jnp.sum(eye * pi, axis=1, keepdims=True))
    qmat = sym * pi
    qmat = qmat - eye * jnp.sum(qmat, axis=1, keepdims=True)
    rate = -jnp.sum(jnp.sum(qmat * eye * pi, axis=1, keepdims=True), axis=0, keepdims=True)
    qmat = (sym * root * root_t + eye * qmat) / rate
    scaled = rates[...] / jnp.mean(rates[...], axis=1, keepdims=True)
    fill = jnp.zeros((1, 2 * taxa - branch.shape[1]), F32)
    lengths = jnp.concatenate([branch[...], fill], axis=1)
    times = [
        lengths[:, h * taxa : (h + 1) * taxa] * scaled[:, k : k + 1]
        for h in range(2)
        for k in range(cats)
    ]
    times = jnp.concatenate(times, axis=1) / 256.0
    batch = cats * taxa

    powers = [qmat]
    dot = functools.partial(jnp.dot, precision=lax.Precision.HIGHEST, preferred_element_type=F32)
    for order in range(2, TAYLOR + 1):
        lo = order // 2
        powers.append(dot(powers[lo - 1], powers[order - lo - 1]))
    fill = jnp.zeros((pad - states, states), F32)
    powers = [jnp.concatenate([p, fill], axis=0) for p in powers]
    def put(dst, i, low, value):
        dst[i, low:, :] = value
        for tile in range(low + 8, pad, 8):
            real = min(8, states - tile)
            mirror = value[tile - low : tile - low + real]
            dst[tile : tile + real, i : i + 1, :] = mirror[:, None, :]

    for i in range(states):
        low = i // 8 * 8
        times_b = jnp.broadcast_to(times, (pad - low, 2 * batch))
        acc = jnp.zeros((pad - low, 2 * batch), F32)
        for order in range(TAYLOR, 0, -1):
            column = jnp.broadcast_to(powers[order - 1][low:, i : i + 1], acc.shape)
            acc = (column + acc) * (times_b * (1.0 / order))
        put(leaf_m, i, low, acc[:, :batch])
        put(inner_m, i, low, acc[:, batch:])

    def square(src, dst, most):
        def part(at, size):
            low = at // 8 * 8
            acc = [src[at + q, low:, :] * 2.0 for q in range(size)]
            for j in range(states):
                right = src[j, low:, :]
                for q in range(size):
                    acc[q] = acc[q] + src[at + q, j : j + 1, :] * right
            for q in range(size):
                put(dst, at + q, low, acc[q])

        pieces = []
        at = 0
        while at < states:
            size = min(most, 8 - at % 8, states - at)
            pieces.append(functools.partial(part, at, size))
            at += size
        return pieces[::-1]

    target = lax.broadcasted_iota(jnp.int32, (group * half, group * states), 1)
    target = (target & (group - 1)) * half + (target >> 3)
    pick = lax.broadcasted_iota(jnp.int32, (group * half, group * states), 0) == target
    picks[...] = pick.astype(F32).astype(BF16)
    chunks = width // chunk
    rounds = SQUARINGS // 2
    groups = taxa // group

    def select(c, g):
        cols = pl.ds(pl.multiple_of(c * chunk, chunk), chunk)
        x = raw[:, pl.ds(g * group, group), cols].reshape(states * group, chunk)
        y = jnp.dot(picks[...], x, preferred_element_type=F32)
        z = y.astype(BF16)
        for one in range(group):
            part = z[one * half : (one + 1) * half]
            leaves[g * group + one, pl.ds(0, half), cols] = part
            leaves[g * group + one, pl.ds(half, half), cols] = part

    def leaf_step(step, carry, beside):
        parts = square(leaf_n, leaf_m, 8) + square(leaf_m, leaf_n, 8)
        total = len(parts)
        work = [(c, g) for c in range(beside) for g in range(groups)]
        if not work:
            while parts:
                parts.pop()()
        else:
            parts.pop()()
        for done, (c, g) in enumerate(work):
            select(step * beside + c, g)
            while parts and (done + 1) * total >= len(work) * (total - len(parts)):
                parts.pop()()
        return carry

    early = rounds // 2
    lax.fori_loop(0, early, functools.partial(leaf_step, beside=0), 0)
    copy.wait()
    late = rounds - early
    lax.fori_loop(0, late, functools.partial(leaf_step, beside=chunks // late), 0)

    sub = lax.broadcasted_iota(jnp.int32, (pad, batch), 0)
    root_w = jnp.concatenate([root_t, jnp.ones((pad - states, 1), F32)], axis=0)
    root_w = jnp.broadcast_to(root_w, (pad, batch))
    over = 1.0 / root_w
    across = lax.broadcasted_iota(jnp.int32, (taxa, LANES), 1)
    many = LANES // pad

    def spread(mat, to, turn):
        for start in range(0, states, many):
            size = min(many, states - start)
            tall = []
            for i in range(start, start + size):
                x = mat[i] * (root_w * over[i : i + 1]) + (sub == i).astype(F32)
                tall.append(x)
            tall.append(jnp.zeros((LANES - size * pad, batch), F32))
            z = jnp.concatenate(tall, axis=0).T
            for q in range(size):
                for k in range(cats):
                    at = k * states if turn else 0
                    part = z[k * taxa : (k + 1) * taxa]
                    shift = (at - q * pad) % LANES
                    if shift:
                        part = pltpu.roll(part, shift, 1)
                    part = jnp.where((across >= at) & (across < at + states), part, 0.0)
                    to[pl.ds((k * states + start + q) * (taxa + 1), taxa), :] = part

    spread(leaf_m, leaf_f, False)
    lane = lax.broadcasted_iota(jnp.int32, (rows, LANES), 1)

    unroll = 8

    def split_leaf(step, carry):
        for n in [step * unroll + u for u in range(unroll)]:
            x = leaf_f[pl.ds(n, rows, stride=taxa + 1), :]
            hi = x.astype(BF16).astype(F32)
            leaf_p[n] = (hi + pltpu.roll(x - hi, half, 1)).astype(BF16)
        return carry

    def split_inner(step, carry):
        for n in [step * unroll + u for u in range(unroll)]:
            x = inner_f[pl.ds(n, rows, stride=taxa + 1), :]
            hi = x.astype(BF16).astype(F32)
            turned = pltpu.roll(hi, rows, 1)
            inner_p[n, :rows, :LANES] = jnp.where(lane < rows, hi, turned).astype(BF16)
            inner_p[n, :rows, LANES:] = jnp.where(lane < 2 * rows - LANES, turned, 0.0).astype(BF16)
            inner_p[n, rows:, :LANES] = (x - hi).astype(BF16)
            inner_p[n, rows:, LANES:] = jnp.zeros((rows, LANES), BF16)
        return carry

    lax.fori_loop(0, taxa // unroll, split_leaf, 0)

    scale[...] = jnp.zeros_like(scale)

    def store(to, node, cols, p):
        hi = p.astype(BF16)
        lo = (p - hi.astype(F32)).astype(BF16)
        to[node, pl.ds(0, rows), cols] = hi
        to[node, pl.ds(rows, rows), cols] = lo

    def messages(node, level, first):
        ids = [children[side, first + node] for side in range(2)]
        if level == 0:
            mats = [leaf_p[child, :, : 2 * half] for child in ids]
            source, base = leaves, 0
        else:
            mats = [inner_p[child - taxa, :, : 2 * rows] for child in ids]
            source, base = levels[level - 1], taxa + first - 2 * (taxa >> (level + 1))
        for c in range(chunks):
            cols = pl.ds(c * chunk, chunk)
            left, right = (
                jnp.dot(mat, source[child - base, :, cols], preferred_element_type=F32)
                for mat, child in zip(mats, ids)
            )
            if level:
                left, right = (side[:rows] + side[rows:] for side in (left, right))
            yield c, cols, left * right

    def at_nodes(step, carry, level, first, each):
        parts, done = [], 0
        if level == 0:
            parts = square(inner_m, inner_n, 8)
            parts = square(inner_n, inner_m, 2) + parts
            total = len(parts)
            every = each * chunks / total
            parts.pop()()
        for u in range(each):
            node = step * each + u
            for c, cols, p in messages(node, level, first):
                if level % 3 == 2:
                    top = jnp.max(p, axis=0, keepdims=True)
                    p = p * (1.0 / top)
                    scale[:, cols] = scale[:, cols] + jnp.log(top)
                store(levels[level], node, cols, p)
                done += 1
                while parts and done >= every * (total - len(parts)):
                    parts.pop()()
        return carry

    first, count, level = 0, taxa // 2, 0
    assert count % rounds == 0
    while count > 1:
        each = min(4, count) if level else count // rounds
        lax.fori_loop(
            0, count // each, functools.partial(at_nodes, level=level, first=first, each=each), 0
        )
        if level == 0:
            spread(inner_m, inner_f, True)
            lax.fori_loop(0, taxa // unroll, split_inner, 0)
        first, count, level = first + count, count // 2, level + 1

    wide = lax.broadcasted_iota(jnp.int32, (rows, states), 0)
    tall = lax.broadcasted_iota(jnp.int32, (rows, states), 1)
    weight = jnp.where(wide % states == tall, pi, 0.0)
    weight = jnp.sum(weight, axis=1, keepdims=True) / cats
    line = lax.broadcasted_iota(jnp.int32, (1, LANES), 1)
    tile = width // slots
    sums = jnp.zeros((1, LANES), F32)
    for c, cols, p in messages(0, level, first):
        lik = jnp.sum(p * weight, axis=0, keepdims=True)
        value = jnp.log(lik) + scale[:, cols]
        for t in range(chunk // tile):
            slot = c * (chunk // tile) + t
            size = counts[0, slot]
            part = jnp.where(line < size, value[:, t * tile : (t + 1) * tile], 0.0)
            site_out[:, pl.ds(slot * tile, tile)] = part
            sum_of = jnp.sum(part, axis=1, keepdims=True)
            gene = jnp.where(size > 0, genes[0, slot], 2 * GROUP_GENES)
            sums = sums + jnp.where(line == gene, sum_of, 0.0)
            sums = sums + jnp.where(line == gene + GROUP_GENES, size.astype(F32), 0.0)
    part_out[...] = jnp.broadcast_to(sums[None], part_out.shape)


def on_device(tips, exchange, freqs, rates, branch, children, slot_gene, site_count):
    taxa, states, width = tips.shape[1:]
    slots = site_count.shape[1]
    cats = rates.shape[0]
    rows = states * cats
    members = lax.axis_size("site")
    groups = lax.axis_size("gene")
    devices = members * groups
    pad = up(states, 8)
    smem = pl.BlockSpec(memory_space=pltpu.SMEM)
    vmem = pl.BlockSpec(memory_space=pltpu.VMEM)
    levels = []
    count = taxa // 2
    while count > 1:
        levels.append(pltpu.VMEM((count, 3 * rows, width), BF16))
        count //= 2
    site, part = pl.pallas_call(
        functools.partial(kernel, (taxa, states, cats, width, slots)),
        out_shape=(
            jax.ShapeDtypeStruct((1, width), F32),
            jax.ShapeDtypeStruct((devices, 1, 2 * GROUP_GENES), F32),
        ),
        in_specs=[smem] * 3 + [vmem] * 4 + [pl.BlockSpec(memory_space=pl.ANY)],
        out_specs=(vmem, vmem),
        scratch_shapes=[
            pltpu.VMEM((states, taxa, width), BF16),
            pltpu.VMEM((states, pad, cats * taxa), F32),
            pltpu.VMEM((states, pad, cats * taxa), F32),
            pltpu.VMEM((states, pad, cats * taxa), F32),
            pltpu.VMEM((states, pad, cats * taxa), F32),
            pltpu.VMEM(((taxa + 1) * (rows + 8), LANES), F32),
            pltpu.VMEM(((taxa + 1) * (rows + 8), LANES), F32),
            pltpu.VMEM((1, width), F32),
            pltpu.SemaphoreType.DMA,
        ],
        compiler_params=pltpu.CompilerParams(vmem_limit_bytes=60 * 1024 * 1024),
        name="prune",
    )(
        children.T,
        site_count,
        slot_gene,
        exchange,
        freqs[None],
        rates[None],
        branch[None],
        tips.transpose(0, 2, 1, 3),
    )
    table = lax.all_to_all(part, ("gene", "site"), split_axis=0, concat_axis=0, tiled=True)
    table = table.reshape(groups, members, 2 * GROUP_GENES)
    mine = lax.dynamic_index_in_dim(table, lax.axis_index("gene"), 0, keepdims=False)
    mine = jnp.sum(mine, axis=0)
    gene = mine[:GROUP_GENES] / mine[GROUP_GENES:]
    total = jnp.sum(table[:, :, :GROUP_GENES]) / (width * members)
    return site, gene[None, :], total


def solution(mesh):
    placed = (
        P("gene", None, None, "site"),
        P(),
        P(),
        P(),
        P(),
        P(),
        P("gene", "site"),
        P("gene", "site"),
    )
    return jax.shard_map(
        on_device,
        mesh=mesh,
        in_specs=placed,
        out_specs=(P("gene", "site"), P("gene", None), P()),
        check_vma=False,
    )
```

```python
import functools

import jax
import jax.numpy as jnp
from jax import lax
from jax.experimental import pallas as pl
from jax.experimental.pallas import tpu as pltpu
from jax.sharding import PartitionSpec as P

GROUP_GENES = 64
TAYLOR = 8
SQUARINGS = 8
LANES = 128
F32 = jnp.float32
BF16 = jnp.bfloat16


def up(value, to):
    return (value + to - 1) // to * to


def kernel(dims, *refs):
    taxa, states, cats, width, slots = dims
    levels = []
    count = taxa // 2
    while count > 1:
        levels.append(pltpu.VMEM((count, 2 * states * cats, width), BF16))
        count //= 2
    rows = states * cats
    half = up(states, 16)
    pl.run_scoped(
        functools.partial(body_of, dims, *refs),
        pltpu.VMEM((taxa, 2 * half, width), BF16),
        pltpu.VMEM((taxa, rows, LANES), BF16),
        pltpu.VMEM((8 * half, 8 * states), BF16),
        pltpu.VMEM((taxa, 2 * rows, 2 * LANES), BF16),
        *levels,
    )


def body_of(
    dims,
    children,
    counts,
    genes,
    exchange,
    freqs,
    rates,
    branch,
    tips,
    site_out,
    part_out,
    raw,
    leaf_m,
    leaf_n,
    inner_m,
    inner_n,
    leaf_f,
    inner_f,
    scale,
    sem,
    leaves,
    leaf_p,
    picks,
    inner_p,
    *levels,
):
    taxa, states, cats, width, slots = dims
    pad = up(states, 8)
    half = up(states, 16)
    rows = states * cats
    chunk = 256
    group = 8
    copy = pltpu.make_async_copy(tips.at[0], raw, sem)
    copy.start()

    row = lax.broadcasted_iota(jnp.int32, (states, states), 0)
    col = lax.broadcasted_iota(jnp.int32, (states, states), 1)
    eye = (row == col).astype(F32)
    sym = (exchange[...] + exchange[...].T) * 0.5 * (1.0 - eye)
    pi = freqs[...] / jnp.sum(freqs[...], axis=1, keepdims=True)
    root = jnp.sqrt(pi)
    root_t = jnp.sqrt(jnp.sum(eye * pi, axis=1, keepdims=True))
    qmat = sym * pi
    qmat = qmat - eye * jnp.sum(qmat, axis=1, keepdims=True)
    rate = -jnp.sum(jnp.sum(qmat * eye * pi, axis=1, keepdims=True), axis=0, keepdims=True)
    qmat = (sym * root * root_t + eye * qmat) / rate
    scaled = rates[...] / jnp.mean(rates[...], axis=1, keepdims=True)
    fill = jnp.zeros((1, 2 * taxa - branch.shape[1]), F32)
    lengths = jnp.concatenate([branch[...], fill], axis=1)
    times = [
        lengths[:, h * taxa : (h + 1) * taxa] * scaled[:, k : k + 1]
        for h in range(2)
        for k in range(cats)
    ]
    times = jnp.concatenate(times, axis=1) / 256.0
    batch = cats * taxa

    powers = [qmat]
    dot = functools.partial(jnp.dot, precision=lax.Precision.HIGHEST, preferred_element_type=F32)
    for order in range(2, TAYLOR + 1):
        lo = order // 2
        powers.append(dot(powers[lo - 1], powers[order - lo - 1]))
    fill = jnp.zeros((pad - states, states), F32)
    powers = [jnp.concatenate([p, fill], axis=0) for p in powers]
    def put(dst, i, low, value):
        dst[i, low:, :] = value
        for tile in range(low + 8, pad, 8):
            real = min(8, states - tile)
            mirror = value[tile - low : tile - low + real]
            dst[tile : tile + real, i : i + 1, :] = mirror[:, None, :]

    for i in range(states):
        low = i // 8 * 8
        times_b = jnp.broadcast_to(times, (pad - low, 2 * batch))
        acc = jnp.zeros((pad - low, 2 * batch), F32)
        for order in range(TAYLOR, 0, -1):
            column = jnp.broadcast_to(powers[order - 1][low:, i : i + 1], acc.shape)
            acc = (column + acc) * (times_b * (1.0 / order))
        put(leaf_m, i, low, acc[:, :batch])
        put(inner_m, i, low, acc[:, batch:])

    def square(src, dst, most):
        def part(at, size):
            low = at // 8 * 8
            acc = [src[at + q, low:, :] * 2.0 for q in range(size)]
            for j in range(states):
                right = src[j, low:, :]
                for q in range(size):
                    acc[q] = acc[q] + src[at + q, j : j + 1, :] * right
            for q in range(size):
                put(dst, at + q, low, acc[q])

        pieces = []
        at = 0
        while at < states:
            size = min(most, 8 - at % 8, states - at)
            pieces.append(functools.partial(part, at, size))
            at += size
        return pieces[::-1]

    target = lax.broadcasted_iota(jnp.int32, (group * half, group * states), 1)
    target = (target & (group - 1)) * half + (target >> 3)
    pick = lax.broadcasted_iota(jnp.int32, (group * half, group * states), 0) == target
    picks[...] = pick.astype(F32).astype(BF16)
    chunks = width // chunk
    rounds = SQUARINGS // 2
    groups = taxa // group

    def select(c, g):
        cols = pl.ds(pl.multiple_of(c * chunk, chunk), chunk)
        x = raw[:, pl.ds(g * group, group), cols].reshape(states * group, chunk)
        y = jnp.dot(picks[...], x, preferred_element_type=F32)
        z = y.astype(BF16)
        for one in range(group):
            part = z[one * half : (one + 1) * half]
            leaves[g * group + one, pl.ds(0, half), cols] = part
            leaves[g * group + one, pl.ds(half, half), cols] = part

    def leaf_step(step, carry, beside):
        parts = square(leaf_n, leaf_m, 8) + square(leaf_m, leaf_n, 8)
        total = len(parts)
        work = [(c, g) for c in range(beside) for g in range(groups)]
        if not work:
            while parts:
                parts.pop()()
        else:
            parts.pop()()
        for done, (c, g) in enumerate(work):
            select(step * beside + c, g)
            while parts and (done + 1) * total >= len(work) * (total - len(parts)):
                parts.pop()()
        return carry

    early = rounds // 2
    lax.fori_loop(0, early, functools.partial(leaf_step, beside=0), 0)
    copy.wait()
    late = rounds - early
    lax.fori_loop(0, late, functools.partial(leaf_step, beside=chunks // late), 0)

    sub = lax.broadcasted_iota(jnp.int32, (pad, batch), 0)
    root_w = jnp.concatenate([root_t, jnp.ones((pad - states, 1), F32)], axis=0)
    root_w = jnp.broadcast_to(root_w, (pad, batch))
    over = 1.0 / root_w
    across = lax.broadcasted_iota(jnp.int32, (taxa, LANES), 1)
    many = LANES // pad

    def spread(mat, to, turn):
        for start in range(0, states, many):
            size = min(many, states - start)
            tall = []
            for i in range(start, start + size):
                x = mat[i] * (root_w * over[i : i + 1]) + (sub == i).astype(F32)
                tall.append(x)
            tall.append(jnp.zeros((LANES - size * pad, batch), F32))
            z = jnp.concatenate(tall, axis=0).T
            for q in range(size):
                for k in range(cats):
                    at = k * states if turn else 0
                    part = z[k * taxa : (k + 1) * taxa]
                    shift = (at - q * pad) % LANES
                    if shift:
                        part = pltpu.roll(part, shift, 1)
                    part = jnp.where((across >= at) & (across < at + states), part, 0.0)
                    to[pl.ds((k * states + start + q) * (taxa + 1), taxa), :] = part

    spread(leaf_m, leaf_f, False)
    lane = lax.broadcasted_iota(jnp.int32, (rows, LANES), 1)

    unroll = 16

    def split_leaf(step, carry):
        for n in [step * unroll + u for u in range(unroll)]:
            x = leaf_f[pl.ds(n, rows, stride=taxa + 1), :]
            hi = x.astype(BF16).astype(F32)
            leaf_p[n] = (hi + pltpu.roll(x - hi, half, 1)).astype(BF16)
        return carry

    def split_inner(step, carry):
        for n in [step * unroll + u for u in range(unroll)]:
            x = inner_f[pl.ds(n, rows, stride=taxa + 1), :]
            hi = x.astype(BF16).astype(F32)
            turned = pltpu.roll(hi, rows, 1)
            inner_p[n, :rows, :LANES] = jnp.where(lane < rows, hi, turned).astype(BF16)
            inner_p[n, :rows, LANES:] = jnp.where(lane < 2 * rows - LANES, turned, 0.0).astype(BF16)
            inner_p[n, rows:, :LANES] = (x - hi).astype(BF16)
            inner_p[n, rows:, LANES:] = jnp.zeros((rows, LANES), BF16)
        return carry

    lax.fori_loop(0, taxa // unroll, split_leaf, 0)

    scale[...] = jnp.zeros_like(scale)

    def store(to, node, cols, p):
        hi = p.astype(BF16)
        lo = (p - hi.astype(F32)).astype(BF16)
        to[node, pl.ds(0, rows), cols] = hi
        to[node, pl.ds(rows, rows), cols] = lo

    def messages(node, level, first):
        ids = [children[side, first + node] for side in range(2)]
        if level == 0:
            mats = [leaf_p[child, :, : 2 * half] for child in ids]
            source, base = leaves, 0
        else:
            mats = [inner_p[child - taxa, :, : 2 * rows] for child in ids]
            source, base = levels[level - 1], taxa + first - 2 * (taxa >> (level + 1))
        for c in range(chunks):
            cols = pl.ds(c * chunk, chunk)
            left, right = (
                jnp.dot(mat, source[child - base, :, cols], preferred_element_type=F32)
                for mat, child in zip(mats, ids)
            )
            if level:
                left, right = (side[:rows] + side[rows:] for side in (left, right))
            yield c, cols, left * right

    def at_nodes(step, carry, level, first, each):
        parts, done = [], 0
        if level == 0:
            parts = square(inner_m, inner_n, 8)
            parts = square(inner_n, inner_m, 2) + parts
            total = len(parts)
            every = each * chunks / total
            parts.pop()()
        for u in range(each):
            node = step * each + u
            for c, cols, p in messages(node, level, first):
                if level % 3 == 2:
                    top = jnp.max(p, axis=0, keepdims=True)
                    p = p * (1.0 / top)
                    scale[:, cols] = scale[:, cols] + jnp.log(top)
                store(levels[level], node, cols, p)
                done += 1
                while parts and done >= every * (total - len(parts)):
                    parts.pop()()
        return carry

    first, count, level = 0, taxa // 2, 0
    assert count % rounds == 0
    while count > 1:
        each = min(4, count) if level else count // rounds
        lax.fori_loop(
            0, count // each, functools.partial(at_nodes, level=level, first=first, each=each), 0
        )
        if level == 0:
            spread(inner_m, inner_f, True)
            lax.fori_loop(0, taxa // unroll, split_inner, 0)
        first, count, level = first + count, count // 2, level + 1

    wide = lax.broadcasted_iota(jnp.int32, (rows, states), 0)
    tall = lax.broadcasted_iota(jnp.int32, (rows, states), 1)
    weight = jnp.where(wide % states == tall, pi, 0.0)
    weight = jnp.sum(weight, axis=1, keepdims=True) / cats
    line = lax.broadcasted_iota(jnp.int32, (1, LANES), 1)
    tile = width // slots
    sums = jnp.zeros((1, LANES), F32)
    for c, cols, p in messages(0, level, first):
        lik = jnp.sum(p * weight, axis=0, keepdims=True)
        value = jnp.log(lik) + scale[:, cols]
        for t in range(chunk // tile):
            slot = c * (chunk // tile) + t
            size = counts[0, slot]
            part = jnp.where(line < size, value[:, t * tile : (t + 1) * tile], 0.0)
            site_out[:, pl.ds(slot * tile, tile)] = part
            sum_of = jnp.sum(part, axis=1, keepdims=True)
            gene = jnp.where(size > 0, genes[0, slot], 2 * GROUP_GENES)
            sums = sums + jnp.where(line == gene, sum_of, 0.0)
            sums = sums + jnp.where(line == gene + GROUP_GENES, size.astype(F32), 0.0)
    part_out[...] = jnp.broadcast_to(sums[None], part_out.shape)


def on_device(tips, exchange, freqs, rates, branch, children, slot_gene, site_count):
    taxa, states, width = tips.shape[1:]
    slots = site_count.shape[1]
    cats = rates.shape[0]
    rows = states * cats
    members = lax.axis_size("site")
    groups = lax.axis_size("gene")
    devices = members * groups
    pad = up(states, 8)
    smem = pl.BlockSpec(memory_space=pltpu.SMEM)
    vmem = pl.BlockSpec(memory_space=pltpu.VMEM)
    levels = []
    count = taxa // 2
    while count > 1:
        levels.append(pltpu.VMEM((count, 3 * rows, width), BF16))
        count //= 2
    site, part = pl.pallas_call(
        functools.partial(kernel, (taxa, states, cats, width, slots)),
        out_shape=(
            jax.ShapeDtypeStruct((1, width), F32),
            jax.ShapeDtypeStruct((devices, 1, 2 * GROUP_GENES), F32),
        ),
        in_specs=[smem] * 3 + [vmem] * 4 + [pl.BlockSpec(memory_space=pl.ANY)],
        out_specs=(vmem, vmem),
        scratch_shapes=[
            pltpu.VMEM((states, taxa, width), BF16),
            pltpu.VMEM((states, pad, cats * taxa), F32),
            pltpu.VMEM((states, pad, cats * taxa), F32),
            pltpu.VMEM((states, pad, cats * taxa), F32),
            pltpu.VMEM((states, pad, cats * taxa), F32),
            pltpu.VMEM(((taxa + 1) * (rows + 8), LANES), F32),
            pltpu.VMEM(((taxa + 1) * (rows + 8), LANES), F32),
            pltpu.VMEM((1, width), F32),
            pltpu.SemaphoreType.DMA,
        ],
        compiler_params=pltpu.CompilerParams(vmem_limit_bytes=60 * 1024 * 1024),
        name="prune",
    )(
        children.T,
        site_count,
        slot_gene,
        exchange,
        freqs[None],
        rates[None],
        branch[None],
        tips.transpose(0, 2, 1, 3),
    )
    table = lax.all_to_all(part, ("gene", "site"), split_axis=0, concat_axis=0, tiled=True)
    table = table.reshape(groups, members, 2 * GROUP_GENES)
    mine = lax.dynamic_index_in_dim(table, lax.axis_index("gene"), 0, keepdims=False)
    mine = jnp.sum(mine, axis=0)
    gene = mine[:GROUP_GENES] / mine[GROUP_GENES:]
    total = jnp.sum(table[:, :, :GROUP_GENES]) / (width * members)
    return site, gene[None, :], total


def solution(mesh):
    placed = (
        P("gene", None, None, "site"),
        P(),
        P(),
        P(),
        P(),
        P(),
        P("gene", "site"),
        P("gene", "site"),
    )
    return jax.shard_map(
        on_device,
        mesh=mesh,
        in_specs=placed,
        out_specs=(P("gene", "site"), P("gene", None), P()),
        check_vma=False,
    )
```
